32 devices in a mesh: gx: 4 (over x, core), gy: 8 (over z, y).
Axes of the slice: x: 2, y: 2, z: 4, core: 2. Of those that a mesh axis runs over, the one named last changes fastest.
Arguments:
- fine_source: bfloat16 [4, 8, 4, 8000], P('gx', 'gy'), may hold values from -6 to 6
- fine_blocks: bfloat16 [3, 12, 20, 20], replicated, may hold values from -0.5 to 0.5
- coarse_blocks: bfloat16 [3, 12, 20, 20], replicated, may hold values from -0.5 to 0.5
- child_filter_matrices: bfloat16 [2, 20, 20], replicated, may hold values from -1 to 1
Outputs:
- fine_result: float32 [4, 8, 4, 8000], P('gx', 'gy')
The draws below stay inside these ranges and needn't reach their ends.
All inputs are finite; a program needn't handle non-finite values.
Results may differ from the reference program's by a relative error of at most 0.013.
Values may be sent and summed in bfloat16 or wider, within the bound.
A program may use at most 64 MiB of HBM per device.

```python
import jax
import jax.numpy as jnp
from jax import lax

K2 = 20
TERMS = 12
FZ = 4
NXF = 4
NYF = 8


def block_levels(key, extent, split, smallest, top_value):
    factor_of = 1.0
    for position, parts in split:
        draws = jax.random.uniform(jax.random.fold_in(jax.random.fold_in(key, 6), position), (parts,), jnp.float32, smallest / len(split), top_value / len(split))
        factor_of = factor_of * jnp.repeat(jnp.exp(draws), extent[position] // parts).reshape((-1,) + (1,) * (len(extent) - 1 - position))
    return factor_of


def bell_draw(rng, extent, spread, most, cuts=(), kind=jnp.bfloat16):
    array = jax.random.normal(rng, extent, jnp.float32) * spread
    if len(cuts) > 0:
        array = block_levels(rng, extent, cuts, -0.22, 0.18) * array
    return jnp.clip(array, min=-most, max=most).astype(kind)


def setup_inputs(seed: int = 0) -> dict:
    keys = jax.random.split(jax.random.key(seed), 5)
    return {
        "fine_source": bell_draw(keys[0], (NXF, NYF, FZ, K2 * K2 * K2), 1.0, 6.0, ((0, 4), (1, 8))),
        "fine_blocks": bell_draw(keys[1], (3, TERMS, K2, K2), (6 * K2) ** -0.5, 0.5),
        "coarse_blocks": bell_draw(keys[2], (3, TERMS, K2, K2), (6 * K2) ** -0.5, 0.5),
        "child_filter_matrices": bell_draw(keys[3], (2, K2, K2), (2 * K2) ** -0.5, 1.0),
    }


def run_pass(values, matrix, coef_axis):
    matrix = matrix.astype(jnp.float32)
    values = values.astype(jnp.float32)
    if coef_axis == 0:
        return jnp.einsum('ca,...ajk->...cjk', matrix, values)
    if coef_axis == 1:
        return jnp.einsum('ca,...iak->...ick', matrix, values)
    return jnp.einsum('ca,...ija->...ijc', matrix, values)


def rounded(values):
    return lax.optimization_barrier(values.astype(jnp.bfloat16))


def shifted(values, grid_axis, offset):
    widths = [(0, 0)] * values.ndim
    widths[grid_axis] = (1, 1)
    padded = jnp.pad(values, widths)
    length = values.shape[grid_axis]
    return lax.slice_in_dim(padded, 1 + offset, 1 + offset + length, axis=grid_axis)


def apply_level(source, blocks):
    def one_term(summed, term_index):
        current = lax.dynamic_index_in_dim(blocks, term_index, 1, keepdims=False)
        lower_block, middle, upper_block = current[0], current[1], current[2]
        base_x = rounded(run_pass(source, middle, 0))
        upper_x = rounded(run_pass(shifted(source, 0, 1), upper_block, 0))
        lower_x = rounded(run_pass(shifted(source, 0, -1), lower_block, 0))
        base_y = rounded(run_pass(base_x, middle, 1))
        upper_y = rounded(run_pass(shifted(base_x, 1, 1), upper_block, 1))
        lower_child_y = rounded(run_pass(shifted(base_x, 1, -1), lower_block, 1))
        upper_xy = rounded(run_pass(upper_x, middle, 1))
        lower_xy = rounded(run_pass(lower_x, middle, 1))
        summed = summed + run_pass(base_y, middle, 2)
        summed = summed + run_pass(shifted(base_y, 2, 1), upper_block, 2)
        summed = summed + run_pass(shifted(base_y, 2, -1), lower_block, 2)
        summed = summed + run_pass(upper_y, middle, 2) + run_pass(lower_child_y, middle, 2)
        summed = summed + run_pass(upper_xy, middle, 2) + run_pass(lower_xy, middle, 2)
        return summed, None

    summed = jnp.zeros(source.shape, jnp.float32)
    summed, _ = lax.scan(one_term, summed, jnp.arange(TERMS, dtype=jnp.int32))
    return summed


def reference(fine_source, fine_blocks, coarse_blocks, child_filter_matrices):
    source = fine_source.reshape(NXF, NYF, FZ, K2, K2, K2)
    fine_term = apply_level(source, fine_blocks)
    scale_factors = child_filter_matrices.astype(jnp.float32)
    children = source.reshape(NXF // 2, 2, NYF // 2, 2, FZ // 2, 2, K2, K2, K2).astype(jnp.float32)
    after_x = rounded(jnp.einsum('ali,xaybzcijk->xaybzcljk', scale_factors, children)).astype(jnp.float32)
    after_y_pass = rounded(jnp.einsum('blj,xaybzcijk->xaybzcilk', scale_factors, after_x)).astype(jnp.float32)
    filtered_coefficients = jnp.einsum('fet,huwgofnmt->huwgofnme', scale_factors, after_y_pass)
    coarse_source = rounded(jnp.sum(filtered_coefficients, axis=(1, 3, 5)))
    coarse_result = rounded(apply_level(coarse_source, coarse_blocks)).astype(jnp.float32)
    grown_x = rounded(jnp.einsum('ail,xyzijk->xayzljk', scale_factors, coarse_result)).astype(jnp.float32)
    grown_y = rounded(jnp.einsum('bjm,xayzljk->xaybzlmk', scale_factors, grown_x)).astype(jnp.float32)
    expanded = jnp.einsum('ckn,xaybzlmk->xaybzclmn', scale_factors, grown_y)
    expanded = expanded.reshape(NXF, NYF, FZ, K2, K2, K2)
    return (fine_term + expanded).reshape(NXF, NYF, FZ, K2 * K2 * K2)
```

```python
import jax
import jax.numpy as jnp
import numpy as np
from jax import lax
from jax.experimental import pallas as pl
from jax.experimental.pallas import tpu as pltpu
from jax.sharding import PartitionSpec as P

BF = jnp.bfloat16
F32 = jnp.float32
PAIR = 2
SUB = 32
LANES = 128


def shifted(block, axis, distance):
    devices = range(lax.axis_size(axis))
    route = [(i - distance, i) for i in devices if i - distance in devices]
    return lax.ppermute(block, axis, route)


def partner(block, axis):
    count = lax.axis_size(axis)
    return lax.ppermute(block, axis, [(i, i ^ 1) for i in range(count)])


SEL_X = np.zeros((4, 5, 3), np.float32)
SEL_X[0, 0, 1] = SEL_X[0, 1, 2] = SEL_X[0, 2, 0] = 1
SEL_X[1, 3, 1] = SEL_X[2, 4, 1] = SEL_X[3, 0, 1] = 1
SEL_Y = np.zeros((2, 4, 3), np.float32)
SEL_Y[0, 0, 1] = SEL_Y[0, 1, 2] = SEL_Y[0, 2, 0] = SEL_Y[1, 3, 1] = 1


def level_mats(blocks, boxes):
    _, terms, n, _ = blocks.shape
    groups = terms // PAIR
    sel_z = np.zeros((2, boxes, boxes, 3), np.float32)
    for z in range(boxes):
        sel_z[0, z, z, 1] = 1
        if z > 0:
            sel_z[1, z, z - 1, 2] = 1
        if z < boxes - 1:
            sel_z[1, z, z + 1, 0] = 1
    first = jnp.einsum("tde,emli->mtldi", jnp.asarray(SEL_X, BF), blocks)
    first = jnp.pad(first, ((0, 0), (0, 0), (0, 24 - n), (0, 0), (0, SUB - n)))
    first = first.reshape(groups, PAIR * 4 * 24, 5 * SUB)
    grouped = blocks.reshape(3, groups, PAIR, n, n)
    second = jnp.einsum(
        "qte,mf,egmlj->gmqlftj", jnp.asarray(SEL_Y, BF), jnp.eye(PAIR, dtype=BF), grouped
    )
    second = jnp.pad(second, ((0, 0),) * 3 + ((0, SUB - n),) + ((0, 0),) * 3)
    second = second.reshape(groups, PAIR * 2 * SUB, PAIR * 4 * n)
    third = jnp.einsum("qzwe,emlk->mqzkwl", jnp.asarray(sel_z, BF), blocks)
    third = third.reshape(terms * 2, boxes * n, boxes * n)
    third = jnp.pad(third, ((0, 0), (0, LANES - boxes * n), (0, LANES - boxes * n)))
    return first, second, third.reshape(terms * 2 * LANES, LANES)


def dot(a, b):
    return jnp.dot(a, b, preferred_element_type=F32)


def level(u, first, second, third, flip, mid, n):
    groups = first.shape[0]
    for g in range(groups):
        slot = flip.at[g % 2]
        width = PAIR * 4 * n
        for j in range(0, n, 2):
            a = dot(first[g], jnp.concatenate([u(j), u(j + 1)], axis=1))
            for h in range(2):
                for t in range(PAIR * 4):
                    slot[pl.ds(t * n + j + h, n, stride=width), :] = a[
                        t * 24 : t * 24 + n, h * LANES : (h + 1) * LANES
                    ]
        for l in range(0, n, 2):
            rhs = jnp.concatenate(
                [slot[l * width : (l + 1) * width, :], slot[(l + 1) * width : (l + 2) * width, :]],
                axis=1,
            ).astype(BF)
            b = dot(second[g], rhs).astype(BF)
            for h in range(2):
                for q in range(PAIR * 2):
                    at = (g * PAIR * 2 + q) * LANES
                    mid[(l + h) * SUB : (l + h + 1) * SUB, at : at + LANES] = b[
                        q * SUB : (q + 1) * SUB, h * LANES : (h + 1) * LANES
                    ]
    return dot(mid[...], third[...])


def single(u, first, second, third, slot, mid, n):
    for j in range(0, n, 2):
        a = dot(first[...], jnp.concatenate([u(j), u(j + 1)], axis=1))
        for h in range(2):
            slot[pl.ds(j + h, n, stride=SUB), :] = a[:n, h * LANES : (h + 1) * LANES]
    for l in range(0, n, 2):
        rhs = jnp.concatenate(
            [slot[l * SUB : l * SUB + n, :], slot[(l + 1) * SUB : (l + 1) * SUB + n, :]], axis=1
        ).astype(BF)
        b = dot(second[...], rhs).astype(BF)
        for h in range(2):
            mid[(l + h) * SUB : (l + h + 1) * SUB, :LANES] = b[:, h * LANES : (h + 1) * LANES]
    return dot(mid[:, :LANES], third[...])


def filter_kernel(u_ref, fx, fy, fz, out, flip, mid):
    n = u_ref.shape[0]
    s = single(lambda j: u_ref[j], fx, fy, fz, flip.at[0], mid, n)
    out[...] = s.reshape(n, SUB, LANES).astype(out.dtype)


def fine_kernel(u_ref, first, second, third, out, flip, mid):
    n = u_ref.shape[0]
    out[...] = level(lambda j: u_ref[j], first, second, third, flip, mid, n).reshape(out.shape)


def coarse_kernel(u_ref, first, second, third, ex, ey, ez, fine, out, flip, mid, res):
    n = u_ref.shape[0]
    s = level(lambda j: u_ref[j], first, second, third, flip, mid, n)
    res[...] = s.reshape(n, SUB, LANES).astype(BF)
    s = single(lambda j: res[j], ex, ey, ez, flip.at[0], mid, n)
    out[...] = fine[...] + s.reshape(out.shape)


def scratch(n, terms):
    return [
        pltpu.VMEM((2, n * PAIR * 4 * n, LANES), F32),
        pltpu.VMEM((n * SUB, terms * 2 * LANES), BF),
    ]


PARAMS = pltpu.CompilerParams(vmem_limit_bytes=60 * 1024 * 1024)


def padded_to(m, rows, cols):
    return jnp.pad(m, ((0, rows - m.shape[0]), (0, cols - m.shape[1])))


def shards(fine_source, fine_blocks, coarse_blocks, filters):
    boxes = fine_source.shape[2]
    parents = boxes // 2
    terms, n = fine_blocks.shape[1], fine_blocks.shape[2]
    raw = fine_source.reshape(boxes, n, n, n)
    own = raw.transpose(2, 1, 0, 3).reshape(n, n, boxes * n)
    own = jnp.pad(own, ((0, 0), (0, SUB - n), (0, LANES - boxes * n)))
    parity_x = lax.axis_index("gx") % 2
    parity_y = lax.axis_index("gy") % 2
    sx = lax.dynamic_index_in_dim(filters, parity_x, 0, keepdims=False)
    sy = lax.dynamic_index_in_dim(filters, parity_y, 0, keepdims=False)
    eye = jnp.eye(parents, dtype=BF)
    fz = jnp.einsum("po,ckn->pcnok", eye, filters).reshape(boxes * n, parents * n)
    ez = jnp.einsum("po,ckn->okpcn", eye, filters).reshape(parents * n, boxes * n)
    fz, ez = padded_to(fz, LANES, LANES), padded_to(ez, LANES, LANES)
    ex, ey = padded_to(sx.T, SUB, SUB), padded_to(sy.T, SUB, n)
    fx, fy = padded_to(sx, SUB, SUB), padded_to(sy, SUB, n)

    grid_out = jax.ShapeDtypeStruct((n, SUB, LANES), BF)
    partial = pl.pallas_call(
        filter_kernel, out_shape=grid_out, scratch_shapes=scratch(n, terms), compiler_params=PARAMS
    )(own, fx, fy, fz)
    sides = [shifted(own, "gx", -1), shifted(own, "gx", 1)]
    sides += [shifted(own, "gy", -1), shifted(own, "gy", 1)]
    fine_u = jnp.concatenate([own] + sides, axis=1)
    half = partial.astype(F32) + partner(partial, "gx").astype(F32)
    parent = (half + partner(half.astype(BF), "gy").astype(F32)).astype(BF)
    near = [shifted(parent, "gy", -2), shifted(parent, "gy", 2)]
    near += [shifted(parent, "gx", -2), shifted(parent, "gx", 2)]
    coarse_u = jnp.concatenate([parent] + near, axis=1)
    fine = pl.pallas_call(
        fine_kernel,
        out_shape=jax.ShapeDtypeStruct((n, SUB, LANES), F32),
        scratch_shapes=scratch(n, terms),
        compiler_params=PARAMS,
        cost_estimate=pl.CostEstimate(flops=4_000_000_000, bytes_accessed=4_000_000, transcendentals=0),
    )(fine_u, *level_mats(fine_blocks, boxes))
    out = pl.pallas_call(
        coarse_kernel,
        out_shape=jax.ShapeDtypeStruct((n, SUB, LANES), F32),
        scratch_shapes=scratch(n, terms) + [pltpu.VMEM((n, SUB, LANES), BF)],
        compiler_params=PARAMS,
    )(coarse_u, *level_mats(coarse_blocks, parents), ex, ey, ez, fine)
    out = out[:, :n, : boxes * n].reshape(n, n, boxes, n).transpose(2, 0, 1, 3)
    return out.reshape(1, 1, boxes, n * n * n)


def solution(mesh):
    in_specs = (P("gx", "gy", None, None), P(), P(), P())
    out_specs = P("gx", "gy", None, None)
    return jax.shard_map(shards, mesh=mesh, in_specs=in_specs, out_specs=out_specs, check_vma=False)
```

```python
import functools

import jax
import jax.numpy as jnp
from jax import lax
from jax.experimental import pallas as pl
from jax.experimental.pallas import tpu as pltpu
from jax.sharding import PartitionSpec as P

BF = jnp.bfloat16
F32 = jnp.float32
PAIR = 2
SUB = 32
LANES = 128


def shifted(block, axis, distance):
    devices = range(lax.axis_size(axis))
    route = [(i - distance, i) for i in devices if i - distance in devices]
    return lax.ppermute(block, axis, route)


def partner(block, axis):
    count = lax.axis_size(axis)
    return lax.ppermute(block, axis, [(i, i ^ 1) for i in range(count)])


TROW = 24


def spread(rows, boxes, n):
    r = lax.broadcasted_iota(jnp.int32, (rows, LANES), 0)
    c = lax.broadcasted_iota(jnp.int32, (rows, LANES), 1)
    return jnp.where((lax.rem(c, n) == r) & (c < boxes * n), 1.0, 0.0).astype(BF)


def spread_t(cols, boxes, n):
    r = lax.broadcasted_iota(jnp.int32, (LANES, cols), 0)
    c = lax.broadcasted_iota(jnp.int32, (LANES, cols), 1)
    return jnp.where((lax.rem(r, n) == c) & (r < boxes * n), 1.0, 0.0).astype(BF)


def box_of(n):
    r = lax.broadcasted_iota(jnp.int32, (LANES, LANES), 0)
    c = lax.broadcasted_iota(jnp.int32, (LANES, LANES), 1)
    return lax.div(r, n), lax.div(c, n)


def tiled(padded, pieces, boxes_in, boxes_out, n):
    wide = dot(padded[:, :SUB].astype(BF), spread(SUB, boxes_in, n)).astype(BF)
    left = spread_t(TROW, boxes_out, n)
    return [dot(left, wide[p * TROW : (p + 1) * TROW]) for p in range(pieces)]


def level_mats(blk, pad, first, second, third, boxes):
    count, n, _ = blk.shape
    terms = count // 3
    pad[...] = jnp.zeros_like(pad)
    second[...] = jnp.zeros_like(second)
    for p in range(count):
        pad[p * TROW : p * TROW + n, :n] = blk[p].astype(F32)
    zero = jnp.zeros((TROW, LANES), F32)
    row, col = box_of(n)
    wide = tiled(pad[...], count, boxes, boxes, n)
    for m in range(terms):
        g, f = divmod(m, PAIR)
        low, mid, up = (pad[(e * terms + m) * TROW : (e * terms + m + 1) * TROW, :] for e in range(3))
        main = mid + pltpu.roll(up, SUB, 1) + pltpu.roll(low, 2 * SUB, 1)
        third_slot = pltpu.roll(mid, 3 * SUB, 1)
        at = f * 4 * TROW
        for t, (x, y) in enumerate([(main, zero), (third_slot, zero), (zero, mid), (mid, zero)]):
            first[g, at + t * TROW : at + (t + 1) * TROW, :LANES] = x
            first[g, at + t * TROW : at + (t + 1) * TROW, LANES:] = y
        at = f * 2 * SUB
        second[g, at : at + TROW, f * LANES : (f + 1) * LANES] = main
        second[g, at + SUB : at + SUB + TROW, f * LANES : (f + 1) * LANES] = third_slot
        at = m * 2 * LANES
        third[:, at : at + LANES] = jnp.where(row == col, wide[terms + m], 0.0).astype(BF)
        third[:, at + LANES : at + 2 * LANES] = (
            jnp.where(col == row + 1, wide[2 * terms + m], 0.0)
            + jnp.where(col == row - 1, wide[m], 0.0)
        ).astype(BF)


def pair_mats(mats, pad, boxes_in, boxes_out, n):
    row, col = box_of(n)
    fine, parent = (col, row) if boxes_in > boxes_out else (row, col)
    for c in range(2):
        pad[c * TROW : c * TROW + n, :n] = mats[c].astype(F32)
    wide = tiled(pad[: 2 * TROW, :], 2, boxes_in, boxes_out, n)
    keep = lax.div(fine, 2) == parent
    even = lax.rem(fine, 2) == 0
    return jnp.where(keep, jnp.where(even, wide[0], wide[1]), 0.0).astype(BF)


def small(mat, pad, at):
    n = mat.shape[0]
    pad[at * SUB : at * SUB + n, :n] = mat.astype(F32)
    return pad[at * SUB : (at + 1) * SUB, :SUB].astype(BF)


def dot_t(a, b):
    return lax.dot_general(a, b, (((1,), (1,)), ((), ())), preferred_element_type=F32)


def dot(a, b):
    return jnp.dot(a, b, preferred_element_type=F32)


def level(u, first, second, third, flip, mid, n):
    groups = first.shape[0]
    width = PAIR * 4 * SUB
    for g in range(groups):
        slot = flip.at[g % 2]
        lhs = first[g][:, : 5 * SUB].astype(BF)
        for j in range(0, n, 2):
            a = dot(lhs, jnp.concatenate([u(j), u(j + 1)], axis=1))
            for h in range(2):
                for t in range(PAIR * 4):
                    slot[pl.ds(t * SUB + j + h, n, stride=width), :] = a[
                        t * TROW : t * TROW + n, h * LANES : (h + 1) * LANES
                    ]
        lhs = second[g].astype(BF)
        for l in range(0, n, 2):
            rhs = jnp.concatenate(
                [slot[l * width : (l + 1) * width, :], slot[(l + 1) * width : (l + 2) * width, :]],
                axis=1,
            ).astype(BF)
            b = dot(lhs, rhs).astype(BF)
            for h in range(2):
                for q in range(PAIR * 2):
                    at = (g * PAIR * 2 + q) * LANES
                    mid[(l + h) * SUB : (l + h + 1) * SUB, at : at + LANES] = b[
                        q * SUB : (q + 1) * SUB, h * LANES : (h + 1) * LANES
                    ]
    return dot_t(mid[...], third[...])


def single(u, first, second, third, slot, mid, n):
    for j in range(0, n, 2):
        a = dot(first, jnp.concatenate([u(j), u(j + 1)], axis=1))
        for h in range(2):
            slot[pl.ds(j + h, n, stride=SUB), :] = a[:n, h * LANES : (h + 1) * LANES]
    for l in range(0, n, 2):
        rhs = jnp.concatenate(
            [slot[l * SUB : l * SUB + n, :], slot[(l + 1) * SUB : (l + 1) * SUB + n, :]], axis=1
        ).astype(BF)
        b = dot(second[:, :n], rhs).astype(BF)
        for h in range(2):
            mid[(l + h) * SUB : (l + h + 1) * SUB, :LANES] = b[:, h * LANES : (h + 1) * LANES]
    return dot_t(mid[:, :LANES], third)


def filter_kernel(px, py, u_ref, filters, out, flip, mid, spare, boxes):
    n = u_ref.shape[0]
    spare[...] = jnp.zeros_like(spare)
    fx, fy = small(filters[px[0]], spare, 0), small(filters[py[0]], spare, 1)
    spare[...] = jnp.zeros_like(spare)
    fz = pair_mats(filters, spare, boxes, boxes // 2, n)
    s = single(lambda j: u_ref[j], fx, fy, fz, flip.at[0], mid, n)
    out[...] = s.reshape(n, SUB, LANES).astype(out.dtype)


def fine_kernel(u_ref, blk, out, flip, mid, pad, first, second, third, boxes):
    n = u_ref.shape[0]
    flip[...] = jnp.zeros_like(flip)
    level_mats(blk, pad, first, second, third, boxes)
    out[...] = level(lambda j: u_ref[j], first, second, third, flip, mid, n).reshape(out.shape)


def coarse_kernel(
    px, py, u_ref, blk, turned, fine, out, flip, mid, pad, first, second, third, res, spare, boxes
):
    n = u_ref.shape[0]
    flip[...] = jnp.zeros_like(flip)
    level_mats(blk, pad, first, second, third, boxes // 2)
    s = level(lambda j: u_ref[j], first, second, third, flip, mid, n)
    res[...] = s.reshape(n, SUB, LANES).astype(BF)
    spare[...] = jnp.zeros_like(spare)
    ex, ey = small(turned[px[0]], spare, 0), small(turned[py[0]], spare, 1)
    spare[...] = jnp.zeros_like(spare)
    ez = pair_mats(turned, spare, boxes // 2, boxes, n)
    s = single(lambda j: res[j], ex, ey, ez, flip.at[0], mid, n)
    out[...] = fine[...] + s.reshape(out.shape)


def scratch(n, terms, whole=True):
    out = [
        pltpu.VMEM((2, n * PAIR * 4 * SUB, LANES), F32),
        pltpu.VMEM((n * SUB, terms * 2 * LANES), BF),
    ]
    if whole:
        groups = terms // PAIR
        out += [
            pltpu.VMEM((3 * terms * TROW, LANES), F32),
            pltpu.VMEM((groups, PAIR * 4 * TROW, 2 * LANES), F32),
            pltpu.VMEM((groups, PAIR * 2 * SUB, 2 * LANES), F32),
            pltpu.VMEM((LANES, terms * 2 * LANES), BF),
        ]
    return out


VM = pl.BlockSpec(memory_space=pltpu.VMEM)
SM = pl.BlockSpec(memory_space=pltpu.SMEM)
SPARE = pltpu.VMEM((2 * SUB, LANES), F32)
PARAMS = pltpu.CompilerParams(vmem_limit_bytes=60 * 1024 * 1024)


def shards(fine_source, fine_blocks, coarse_blocks, filters):
    boxes = fine_source.shape[2]
    terms, n = fine_blocks.shape[1], fine_blocks.shape[2]
    raw = fine_source.reshape(boxes, n, n, n)
    own = raw.transpose(2, 1, 0, 3).reshape(n, n, boxes * n)
    own = jnp.pad(own, ((0, 0), (0, SUB - n), (0, LANES - boxes * n)))
    parity_x = lax.axis_index("gx") % 2
    parity_y = lax.axis_index("gy") % 2
    px, py = parity_x.reshape(1), parity_y.reshape(1)
    turned = filters.swapaxes(1, 2)
    grid_out = jax.ShapeDtypeStruct((n, SUB, LANES), BF)
    partial = pl.pallas_call(
        functools.partial(filter_kernel, boxes=boxes),
        out_shape=grid_out,
        in_specs=[SM, SM, VM, VM],
        out_specs=VM,
        scratch_shapes=scratch(n, terms, False) + [SPARE],
        compiler_params=PARAMS,
    )(px, py, own, filters)
    sides = [shifted(own, "gx", -1), shifted(own, "gx", 1)]
    sides += [shifted(own, "gy", -1), shifted(own, "gy", 1)]
    fine_u = jnp.concatenate([own] + sides, axis=1)
    half = partial.astype(F32) + partner(partial, "gx").astype(F32)
    parent = (half + partner(half.astype(BF), "gy").astype(F32)).astype(BF)
    near = [shifted(parent, "gy", -2), shifted(parent, "gy", 2)]
    near += [shifted(parent, "gx", -2), shifted(parent, "gx", 2)]
    coarse_u = jnp.concatenate([parent] + near, axis=1)
    fine = pl.pallas_call(
        functools.partial(fine_kernel, boxes=boxes),
        out_shape=jax.ShapeDtypeStruct((n, SUB, LANES), F32),
        scratch_shapes=scratch(n, terms),
        compiler_params=PARAMS,
        cost_estimate=pl.CostEstimate(flops=4_000_000_000, bytes_accessed=4_000_000, transcendentals=0),
    )(fine_u, fine_blocks.reshape(3 * terms, n, n))
    out = pl.pallas_call(
        functools.partial(coarse_kernel, boxes=boxes),
        in_specs=[SM, SM, VM, VM, VM, VM],
        out_specs=VM,
        out_shape=jax.ShapeDtypeStruct((n, SUB, LANES), F32),
        scratch_shapes=scratch(n, terms) + [pltpu.VMEM((n, SUB, LANES), BF), SPARE],
        compiler_params=PARAMS,
    )(px, py, coarse_u, coarse_blocks.reshape(3 * terms, n, n), turned, fine)
    out = out[:, :n, : boxes * n].reshape(n, n, boxes, n).transpose(2, 0, 1, 3)
    return out.reshape(1, 1, boxes, n * n * n)


def solution(mesh):
    in_specs = (P("gx", "gy", None, None), P(), P(), P())
    out_specs = P("gx", "gy", None, None)
    return jax.shard_map(shards, mesh=mesh, in_specs=in_specs, out_specs=out_specs, check_vma=False)
```
